256 devices in a mesh: wide: 64 (over y, z, core), layer: 4 (over x).
Axes of the slice: x: 4, y: 4, z: 8, core: 2. Of those that a mesh axis runs over, the one named last changes fastest.
Arguments:
- amplitudes: bfloat16 [8192, 4, 4096], P('wide', 'layer'), may hold values from -6 to 6
- tile_pos: int32 [8192, 4], P('wide', 'layer'), may hold values from 0 to 255, as said below
- tile_count: int32 [64, 4], P('wide', 'layer'), may hold values from 16 to 128, as said below
- integrals: bfloat16 [4096, 4096], P('wide', 'layer'), may hold values from -0.09375 to 0.09375
Outputs:
- residual: bfloat16 [65536, 4096], P('wide', 'layer')
The draws below stay inside these ranges and needn't reach their ends.
Inputs may be any that keep to these rules, and one draw needn't show every extreme that they name: `tile_pos`: for each owner and layer the 128 values are distinct; value p names row tile p // 16 of the owner's 16 and contraction tile p % 16 of the layer's 16. `tile_count`: the leading slots of an owner and layer are the listed ones; some owner and layer lists all 128.
All inputs are finite; a program needn't handle non-finite values.
Results may differ from the reference program's by a relative error of at most 0.009.
Values may be sent and summed in bfloat16 or wider, within the bound.
No kernel may reach another device: no remote copies, remote signals or barrier semaphores. Data moves between devices by JAX's collectives and lax.ppermute only.
A program may use at most 64 MiB of HBM per device.

```python
import jax
import jax.numpy as jnp
from jax import lax

TILE = 64
N = 4096
ROW_TILES = 16
LAYER_TILES = 16
SLOTS = 128
ROWS = 65536
K = 4096
N_WIDE = 64
N_LAYER = 4


def shuffle_slots(single_key):
    return jax.random.permutation(single_key, SLOTS)


def draw_tile_pos(key, part):
    owners = N_WIDE * N_LAYER
    key_list = jax.random.split(jax.random.fold_in(key, 11), owners)
    orders = jax.vmap(shuffle_slots)(key_list).astype(jnp.int32)
    halves = jax.random.randint(jax.random.fold_in(key, 12), (owners, SLOTS), 0, 2).astype(jnp.int32)
    chosen = jax.random.randint(jax.random.fold_in(key, 13), (), 0, owners)
    forced = jnp.where(orders == 0, 0, 1).astype(jnp.int32)
    halves = jnp.where(jnp.arange(owners)[:, None] == chosen, forced, halves)
    places = 2 * orders + halves
    places = places.reshape(N_WIDE, N_LAYER, SLOTS).transpose(0, 2, 1)
    return places.reshape(N_WIDE * SLOTS, N_LAYER).astype(jnp.int32)


def draw_tile_count(key, part):
    owners = N_WIDE * N_LAYER
    lowest = max(1, SLOTS // 8)
    counts = jax.random.randint(jax.random.fold_in(key, 21), (owners,), lowest, SLOTS // 2 + SLOTS // 4 + 1)
    chosen = jax.random.randint(jax.random.fold_in(key, 22), (), 0, owners)
    offset = jax.random.randint(jax.random.fold_in(key, 23), (), 0, owners - 1)
    second = (chosen + 1 + offset) % owners
    counts = jnp.where(jnp.arange(owners) == second, lowest, counts)
    counts = jnp.where(jnp.arange(owners) == chosen, SLOTS, counts)
    return counts.reshape(N_WIDE, N_LAYER).astype(jnp.int32)


def levels(rng, shape, pieces, smallest, largest):
    factor_of = 1.0
    for position, shards_of in pieces:
        steps = jax.random.uniform(jax.random.fold_in(jax.random.fold_in(rng, 6), position), (shards_of,), jnp.float32, smallest / len(pieces), largest / len(pieces))
        factor_of = factor_of * jnp.repeat(jnp.exp(steps), shape[position] // shards_of).reshape((-1,) + (1,) * (len(shape) - 1 - position))
    return factor_of


def noise(stream_key, shape, width, bound, cuts=(), kind=jnp.bfloat16):
    gain = levels(stream_key, shape, cuts, -0.22, 0.18) if cuts else 1.0
    array = jax.random.normal(stream_key, shape, jnp.float32) * width * gain
    return jnp.minimum(jnp.maximum(array, -bound), bound).astype(kind)


def setup_inputs(seed: int = 0) -> dict:
    splits = jax.random.split(jax.random.key(seed), 5)
    return {
        "amplitudes": noise(splits[0], (N_WIDE * SLOTS, N_LAYER, TILE * TILE), 1.0, 6.0, ((0, 64), (1, 4))),
        "tile_pos": draw_tile_pos(jax.random.fold_in(splits[4], 71), 0),
        "tile_count": draw_tile_count(jax.random.fold_in(splits[4], 71), 0),
        "integrals": noise(splits[3], (K, N), K ** -0.5, 0.09375, ((0, 64), (1, 4))),
    }


def reference(amplitudes, tile_pos, tile_count, integrals):
    integral_tiles = integrals.reshape(N_LAYER * LAYER_TILES, TILE, N)
    amplitude_all = amplitudes.reshape(N_WIDE, SLOTS, N_LAYER, TILE, TILE)
    position_all = tile_pos.reshape(N_WIDE, SLOTS, N_LAYER)

    def ladder_owner(owner_inputs):
        amplitude_tiles, positions, listed_count = owner_inputs
        slot_index = jnp.arange(SLOTS, dtype=jnp.int32)
        layer_index = jnp.arange(N_LAYER, dtype=jnp.int32)
        listed = slot_index[:, None] < listed_count[None, :]
        contraction_tile = (positions % LAYER_TILES + LAYER_TILES * layer_index[None, :]).astype(jnp.int32)
        row_tile = (positions // LAYER_TILES).astype(jnp.int32)
        picked = integral_tiles[contraction_tile.reshape(-1)].astype(jnp.float32)
        picked = picked.reshape(SLOTS, N_LAYER, TILE, N)
        masked = jnp.where(listed[:, :, None, None], amplitude_tiles.astype(jnp.float32), jnp.zeros((), jnp.float32))
        products = jnp.einsum("slij,sljn->slin", masked, picked)
        row_hot = (row_tile[:, :, None] == jnp.arange(ROW_TILES, dtype=jnp.int32)[None, None, :]).astype(jnp.float32)
        layered = jnp.einsum("slr,slin->lrin", row_hot, products)
        rounded = lax.optimization_barrier(layered.astype(jnp.bfloat16)).astype(jnp.float32)
        summed = jnp.sum(rounded, axis=0)
        return summed.reshape(ROW_TILES * TILE, N).astype(jnp.bfloat16)

    owner_rows = lax.map(ladder_owner, (amplitude_all, position_all, tile_count))
    return owner_rows.reshape(ROWS, N)
```

```python
import functools

import jax
import jax.numpy as jnp
import numpy as np
from jax import lax
from jax.experimental import pallas as pl
from jax.experimental.pallas import tpu as pltpu
from jax.sharding import PartitionSpec as P


Y, Z, CORES, LAYERS = 4, 8, 2, 4
HALF = 32 * 64
META = 16
ABSENT = 256
MIB = 1 << 20


UNIT_BY_DZ = {0: 0, 7: 1, 1: 2, 6: 3, 2: 4, 5: 5, 3: 6, 4: 7}
PLACE_BY_DY = {0: 0, 3: 1, 1: 2, 2: 3}
HALF_BY_DZ = {0: (0, 0), 7: (0, 1), 1: (0, 2), 6: (0, 3), 2: (1, 0), 5: (1, 1), 3: (1, 2), 4: (1, 3)}
UNIT_BY_HALF_DY = {(0, 0): 0, (0, 3): 1, (1, 1): 2, (0, 2): 3, (1, 2): 4, (1, 3): 5, (0, 1): 6, (1, 0): 7}


def place_table():
    table = np.zeros((Y, Z, CORES, LAYERS, LAYERS, 16), np.int32)
    for y, z, c, x, dx, t in np.ndindex(*table.shape):
        layer = (x + dx) % LAYERS
        dy, dz, core = (layer - y) % Y, (t // 2 - z) % Z, t % 2
        if core == 0:
            unit, place = UNIT_BY_DZ[dz], PLACE_BY_DY[dy]
        else:
            half, place = HALF_BY_DZ[dz]
            unit = UNIT_BY_HALF_DY[half, dy]
        table[y, z, c, x, dx, t] = (unit + (0 if core == c else 8)) * 4 + place
    return table.reshape(Y * Z * CORES, LAYERS, LAYERS, 16)


def vmem():
    return pl.BlockSpec(memory_space=pltpu.VMEM)


def smem():
    return pl.BlockSpec(memory_space=pltpu.SMEM)


def prep_kernel(count_ref, amp_ref, pos_ref, low_ref, high_ref, wide_ref):
    left = lax.broadcasted_iota(jnp.int32, (64, 128), 1) < 64
    for t in range(32):
        cols = slice(t * 128, (t + 1) * 128)
        xa = amp_ref[0:64, cols].astype(jnp.float32)
        xb = amp_ref[64:128, cols].astype(jnp.float32)
        even = jnp.where(left, xa, pltpu.roll(xb, 64, 1))
        odd = jnp.where(left, pltpu.roll(xa, 64, 1), xb)
        wide_ref[2 * t * 64 : (2 * t + 1) * 64, :] = even
        wide_ref[(2 * t + 1) * 64 : (2 * t + 2) * 64, :] = odd
    slot = lax.broadcasted_iota(jnp.int32, (1, 128), 1)
    code = jnp.where(slot < count_ref[0, 0], pos_ref[...], ABSENT).astype(jnp.float32)
    code = jnp.broadcast_to(code, (META, 128)).astype(jnp.bfloat16)
    for half, ref in enumerate((low_ref, high_ref)):
        for s in range(32):
            rows = wide_ref[pl.ds(half * 32 + s, 64, stride=64), :]
            ref[s * 64 : (s + 1) * 64, :] = rows.astype(jnp.bfloat16)
        ref[HALF:, :] = code


def prep(count, amplitudes, positions):
    out = jax.ShapeDtypeStruct((HALF + META, 128), jnp.bfloat16)
    return pl.pallas_call(
        prep_kernel,
        out_shape=(out, out),
        in_specs=[smem(), vmem(), vmem()],
        out_specs=(vmem(), vmem()),
        scratch_shapes=[pltpu.VMEM((4096, 128), jnp.float32)],
        compiler_params=pltpu.CompilerParams(vmem_limit_bytes=12 * MIB),
        name="prep",
    )(count, amplitudes, positions)


def place_kernel(halves, table_ref, *refs):
    sources, (dense_ref, code_v, code_s, sem) = refs[: len(halves)], refs[len(halves) :]

    def zero(k, carry):
        dense_ref[k] = jnp.zeros((1024, 128), jnp.bfloat16)
        return carry

    lax.fori_loop(0, 32, zero, 0)
    side = jnp.where(lax.broadcasted_iota(jnp.int32, (64, 128), 1) < 64, 0, 1)
    for source_ref, (piece, half) in zip(sources, halves):
        code_v[...] = source_ref[HALF:, :].astype(jnp.float32).astype(jnp.int32)[0:8]
        copy = pltpu.make_async_copy(code_v, code_s, sem)
        copy.start()
        copy.wait()
        for h in range(2):

            def one(s, carry):
                code = code_s[0, h * 64 + half * 32 + s]

                @pl.when(code < ABSENT)
                def _():
                    u = table_ref[piece, code & 15]
                    q = u & 1
                    block = source_ref[pl.ds(pl.multiple_of(s * 64, 64), 64), :]
                    swapped = jnp.concatenate([block[:, 64:], block[:, :64]], axis=1)
                    block = jnp.where(q == h, block, swapped)
                    rows = pl.ds(pl.multiple_of((code >> 4) * 64, 64), 64)
                    dense_ref[u >> 1, rows, :] = jnp.where(side == q, block, dense_ref[u >> 1, rows, :])

                return carry

            lax.fori_loop(0, 32, one, 0)


def place(table, sources, halves):
    return pl.pallas_call(
        functools.partial(place_kernel, halves),
        out_shape=jax.ShapeDtypeStruct((32, 1024, 128), jnp.bfloat16),
        in_specs=[smem()] + [vmem()] * len(sources),
        out_specs=vmem(),
        scratch_shapes=[pltpu.VMEM((8, 128), jnp.int32), pltpu.SMEM((8, 128), jnp.int32), pltpu.SemaphoreType.DMA],
        compiler_params=pltpu.CompilerParams(vmem_limit_bytes=12 * MIB),
        name="place",
    )(table, *sources)


def product_kernel(units, has_total, a_ref, b_ref, *refs):
    blocks, rest = refs[: len(units)], refs[len(units) :]
    out_ref = rest[-1]

    def rows_of(i, carry):
        rows = pl.ds(pl.multiple_of(i * 256, 256), 256)
        for n in range(4):
            cols = slice(n * 256, (n + 1) * 256)
            total = rest[0][rows, cols] if has_total else None
            for k, block in zip(units, blocks):
                left = [a_ref[j, rows, :] + b_ref[j, rows, :] for j in (2 * k, 2 * k + 1)]
                part = jnp.dot(jnp.concatenate(left, axis=1), block[:, cols], preferred_element_type=jnp.float32)
                total = part if total is None else total + part
            out_ref[rows, cols] = total.astype(out_ref.dtype)
        return carry

    lax.fori_loop(0, 4, rows_of, 0)


def product(a, b, blocks, units, total, dtype):
    args = [a, b, *blocks] + ([] if total is None else [total])
    return pl.pallas_call(
        functools.partial(product_kernel, units, total is not None),
        out_shape=jax.ShapeDtypeStruct((1024, 1024), dtype),
        in_specs=[vmem()] * len(args),
        out_specs=vmem(),
        compiler_params=pltpu.CompilerParams(vmem_limit_bytes=12 * MIB),
        name="product",
    )(*args)


def pairs(move0, move1):
    out = []
    for y, z, c in np.ndindex(Y, Z, CORES):
        move = (move0, move1)[c]
        if move is not None:
            target = ((y + move[0]) % Y * Z + (z + move[1]) % Z) * CORES + c
            out.append(((y * Z + z) * CORES + c, int(target)))
    return out


def send(value, move0, move1):
    return lax.ppermute(value, "wide", pairs(move0, move1))


def swap(value):
    return lax.ppermute(value, "wide", [(i, i ^ 1) for i in range(Y * Z * CORES)])


def shift(value, step):
    return lax.ppermute(value, "layer", [(i, (i + step) % LAYERS) for i in range(LAYERS)])


def body(amplitudes, tile_pos, tile_count, integrals):
    wide = lax.axis_index("wide")
    core0 = wide % 2 == 0
    table = jnp.asarray(place_table())[wide, lax.axis_index("layer")]

    near = [
        send(integrals, (1, 0), (0, 1)),
        send(integrals, (-1, 0), (0, -1)),
        send(integrals, (2, 0), (0, 2)),
    ]
    low, high = prep(tile_count, amplitudes[:, 0, :], tile_pos.reshape(1, 128))
    left_low, right_high = shift(low, 1), shift(high, -1)
    left_high, right_low = shift(high, 1), shift(low, -1)
    far = [send(integrals, None, (0, d)) for d in (-2, 3, -3, 4)]

    unit0 = jnp.concatenate([integrals, *near], axis=0)
    r1p = send(unit0, (0, 1), (1, 0))
    unit1 = jnp.concatenate(far, axis=0)
    other = jnp.where(core0, unit0, unit1)
    r1m = send(other, (0, -1), (-1, 0))
    r2p, r2m = send(r1p, (0, 1), (1, 0)), send(r1m, (0, -1), (-1, 0))
    far_low, far_high = shift(left_low, 1), shift(right_high, -1)
    r3p = send(jnp.where(core0, r2p, other), (0, 1), (1, 0))
    r3m = send(jnp.where(core0, r2m, unit0), (0, -1), (-1, 0))
    r4 = send(r3p, (0, 1), None)
    last = jnp.where(core0, r4, other)

    mine = [unit0, r1p, r1m, r2p, r2m, r3p, r3m, last]
    theirs = [swap(unit) for unit in mine]
    dense3 = place(
        table,
        [low, high, left_low, right_high, left_high, right_low],
        ((0, 0), (0, 1), (3, 0), (1, 1), (3, 1), (1, 0)),
    )
    dense1 = place(table, [far_low, far_high], ((2, 0), (2, 1)))
    first = (0, 1, 2, 3, 4)
    early = [mine[i] for i in first] + [theirs[i] for i in first]
    total = product(dense3, dense1, early, first + tuple(8 + i for i in first), None, jnp.float32)
    rest = (5, 6, 7)
    late = [mine[i] for i in rest] + [theirs[i] for i in rest]
    return product(dense3, dense1, late, rest + tuple(8 + i for i in rest), total, jnp.bfloat16)


def solution(mesh):
    in_specs = (
        P("wide", "layer", None),
        P("wide", "layer"),
        P("wide", "layer"),
        P("wide", "layer"),
    )
    return jax.shard_map(body, mesh=mesh, in_specs=in_specs, out_specs=P("wide", "layer"), check_vma=False)
```

```python
import functools

import jax
import jax.numpy as jnp
import numpy as np
from jax import lax
from jax.experimental import pallas as pl
from jax.experimental.pallas import tpu as pltpu
from jax.sharding import PartitionSpec as P


Y, Z, CORES, LAYERS = 4, 8, 2, 4
HALF = 32 * 64
META = 16
ABSENT = 256
UNROLL = 8
MIB = 1 << 20


UNIT_BY_DZ = {0: 0, 7: 1, 1: 2, 6: 3, 2: 4, 5: 5, 3: 6, 4: 7}
PLACE_BY_DY = {0: 0, 3: 1, 2: 2, 1: 3}
HALF_BY_DZ = {0: (0, 0), 7: (0, 1), 6: (0, 2), 5: (0, 3), 2: (1, 0), 1: (1, 1), 4: (1, 2), 3: (1, 3)}
UNIT_BY_HALF_DY = {(0, 0): 0, (0, 3): 1, (1, 1): 2, (0, 2): 3, (1, 2): 4, (0, 1): 5, (1, 3): 6, (1, 0): 7}


def place_table():
    table = np.zeros((Y, Z, CORES, LAYERS, LAYERS, 16), np.int32)
    for y, z, c, x, dx, t in np.ndindex(*table.shape):
        layer = (x + dx) % LAYERS
        dy, dz, core = (layer - y) % Y, (t // 2 - z) % Z, t % 2
        if core == 0:
            unit, place = UNIT_BY_DZ[dz], PLACE_BY_DY[dy]
        else:
            half, place = HALF_BY_DZ[dz]
            unit = UNIT_BY_HALF_DY[half, dy]
        table[y, z, c, x, dx, t] = (unit + (0 if core == c else 8)) * 4 + place
    core = np.broadcast_to(np.arange(CORES, dtype=np.int32)[:, None, None, None], (Y, Z, CORES, LAYERS, 1, 16))
    return np.concatenate([table, core], axis=4).reshape(Y * Z * CORES, LAYERS, LAYERS + 1, 16)


def vmem():
    return pl.BlockSpec(memory_space=pltpu.VMEM)


def smem():
    return pl.BlockSpec(memory_space=pltpu.SMEM)


def prep_kernel(table_ref, count_ref, amp_hbm, pos_ref, low_ref, high_ref, amp_ref, wide_ref, sems):
    copies = []
    for n in range(4):
        cols = pl.ds(n * 1024, 1024)
        copies.append(pltpu.make_async_copy(amp_hbm.at[:, cols], amp_ref.at[:, cols], sems.at[n]))
        copies[n].start()
    left = lax.broadcasted_iota(jnp.int32, (64, 128), 1) < 64
    for t in range(32):
        if t % 8 == 0:
            copies[t // 8].wait()
        cols = slice(t * 128, (t + 1) * 128)
        xa = amp_ref[0:64, cols].astype(jnp.float32)
        xb = amp_ref[64:128, cols].astype(jnp.float32)
        even = jnp.where(left, xa, pltpu.roll(xb, 64, 1))
        odd = jnp.where(left, pltpu.roll(xa, 64, 1), xb)
        wide_ref[2 * t * 64 : (2 * t + 1) * 64, :] = even
        wide_ref[(2 * t + 1) * 64 : (2 * t + 2) * 64, :] = odd
    slot = lax.broadcasted_iota(jnp.int32, (1, 128), 1)
    code = jnp.where(slot < count_ref[0, 0], pos_ref[...], ABSENT).astype(jnp.float32)
    code = jnp.broadcast_to(code, (META, 128)).astype(jnp.bfloat16)
    for half, ref in enumerate((low_ref, high_ref)):
        for s in range(32):
            rows = wide_ref[pl.ds(half * 32 + s, 64, stride=64), :]
            ref[s * 64 : (s + 1) * 64, :] = rows.astype(jnp.bfloat16)
        ref[HALF:, :] = code


def prep(table, count, amplitudes, positions):
    out = jax.ShapeDtypeStruct((HALF + META, 128), jnp.bfloat16)
    low, high = pl.pallas_call(
        prep_kernel,
        out_shape=(out, out),
        in_specs=[smem(), smem(), pl.BlockSpec(memory_space=pltpu.HBM), vmem()],
        out_specs=(vmem(), vmem()),
        scratch_shapes=[
            pltpu.VMEM((128, 4096), jnp.bfloat16),
            pltpu.VMEM((4096, 128), jnp.float32),
            pltpu.SemaphoreType.DMA((4,)),
        ],
        compiler_params=pltpu.CompilerParams(vmem_limit_bytes=6 * MIB),
        name="prep",
    )(table, count, amplitudes, positions)
    return low, high


def join_kernel(a_ref, b_ref, out_ref):
    out_ref[: a_ref.shape[0]] = a_ref[...]
    out_ref[a_ref.shape[0] :] = b_ref[...]


def join(a, b):
    out = pl.pallas_call(
        join_kernel,
        out_shape=jax.ShapeDtypeStruct((a.shape[0] + b.shape[0], a.shape[1]), a.dtype),
        in_specs=[vmem(), vmem()],
        out_specs=vmem(),
        compiler_params=pltpu.CompilerParams(vmem_limit_bytes=2 * MIB),
        name="join",
    )(a, b)
    return out


def place_kernel(halves, given, table_ref, *refs):
    sources, rest = refs[: len(halves)], refs[len(halves) :]
    if given:
        dense_ref, _, code_v, code_s, sem = rest
    else:
        dense_ref, code_v, code_s, sem = rest

        def zero(k, carry):
            dense_ref[k] = jnp.zeros((1024, 128), jnp.bfloat16)
            return carry

        lax.fori_loop(0, 32, zero, 0)
    side = jnp.where(lax.broadcasted_iota(jnp.int32, (64, 128), 1) < 64, 0, 1)
    for n, source_ref in enumerate(sources):
        code_v[8 * n : 8 * n + 8] = source_ref[HALF:, :].astype(jnp.float32).astype(jnp.int32)[0:8]
    copy = pltpu.make_async_copy(code_v, code_s, sem)
    copy.start()
    copy.wait()
    for n, (source_ref, (piece, half)) in enumerate(zip(sources, halves)):

        def trip(first, carry):
            for j in range(UNROLL):
                s = first * UNROLL + j
                block = source_ref[pl.ds(pl.multiple_of(s * 64, 64), 64), :]
                swapped = jnp.concatenate([block[:, 64:], block[:, :64]], axis=1)
                for h in range(2):
                    code = code_s[8 * n, h * 64 + half * 32 + s]
                    u = table_ref[piece, code & 15]
                    q = u & 1
                    tile = jnp.where(q == h, block, swapped)
                    k = jnp.where(code < ABSENT, u >> 1, 32)
                    rows = pl.ds(pl.multiple_of((code & 240) * 4, 64), 64)
                    dense_ref[k, rows, :] = jnp.where(side == q, tile, dense_ref[k, rows, :])
            return carry

        lax.fori_loop(0, 32 // UNROLL, trip, 0)


def place(table, sources, halves, dense=None):
    given = [] if dense is None else [dense]
    n = len(sources)
    out = pl.pallas_call(
        functools.partial(place_kernel, halves, bool(given)),
        out_shape=jax.ShapeDtypeStruct((33, 1024, 128), jnp.bfloat16),
        in_specs=[smem()] + [vmem()] * (n + len(given)),
        out_specs=vmem(),
        input_output_aliases={n + 1: 0} if given else {},
        scratch_shapes=[
            pltpu.VMEM((8 * n, 128), jnp.int32),
            pltpu.SMEM((8 * n, 128), jnp.int32),
            pltpu.SemaphoreType.DMA,
        ],
        compiler_params=pltpu.CompilerParams(vmem_limit_bytes=16 * MIB),
        name="place",
    )(table, *sources, *given)
    return out


def product_kernel(units, has_total, table_ref, dense_ref, *refs):
    count = sum(choices for _, choices in units)
    total_ref = refs[count] if has_total else None
    out_ref, block_ref, sems = refs[-3:]
    waits = []
    at = 0
    for n, (_, choices) in enumerate(units):
        copies = [pltpu.make_async_copy(refs[at + j], block_ref.at[n], sems.at[n]) for j in range(choices)]
        at += choices
        waits.append(copies[0])
        if choices == 1:
            copies[0].start()
        else:
            for j, copy in enumerate(copies):
                pl.when(table_ref[LAYERS, 0] == j)(copy.start)

    def rows_of(i, carry):
        rows = pl.ds(pl.multiple_of(i * 512, 512), 512)
        for n in range(4):
            cols = slice(n * 256, (n + 1) * 256)
            total = total_ref[rows, cols] if has_total else None
            for at, (k, _) in enumerate(units):
                if n == 0:
                    pl.when(i == 0)(waits[at].wait)
                left = jnp.concatenate([dense_ref[2 * k, rows, :], dense_ref[2 * k + 1, rows, :]], axis=1)
                part = jnp.dot(left, block_ref[at, :, cols], preferred_element_type=jnp.float32)
                total = part if total is None else total + part
            out_ref[rows, cols] = total.astype(out_ref.dtype)
        return carry

    lax.fori_loop(0, 2, rows_of, 0)


def product(table, dense, blocks, total, dtype):
    arrays = [array for _, choices in blocks for array in choices]
    units = tuple((k, len(choices)) for k, choices in blocks)
    totals = [] if total is None else [total]
    return pl.pallas_call(
        functools.partial(product_kernel, units, bool(totals)),
        out_shape=jax.ShapeDtypeStruct((1024, 1024), dtype),
        in_specs=[smem(), vmem()] + [pl.BlockSpec(memory_space=pl.ANY)] * len(arrays) + [vmem()] * len(totals),
        out_specs=vmem(),
        scratch_shapes=[pltpu.VMEM((len(units), 256, 1024), jnp.bfloat16), pltpu.SemaphoreType.DMA((len(units),))],
        compiler_params=pltpu.CompilerParams(vmem_limit_bytes=16 * MIB),
        name="product",
    )(table, dense, *arrays, *totals)


def pairs(move0, move1):
    out = []
    for y, z, c in np.ndindex(Y, Z, CORES):
        move = (move0, move1)[c]
        if move is not None:
            target = ((y + move[0]) % Y * Z + (z + move[1]) % Z) * CORES + c
            out.append(((y * Z + z) * CORES + c, int(target)))
    return out


def send(value, move0, move1):
    return lax.ppermute(value, "wide", pairs(move0, move1))


def swap(value, cores=(0, 1)):
    return lax.ppermute(value, "wide", [(i, i ^ 1) for i in range(Y * Z * CORES) if i % 2 in cores])


def shift(value, step):
    return lax.ppermute(value, "layer", [(i, (i + step) % LAYERS) for i in range(LAYERS)])


def steps(amplitudes, tile_pos, tile_count, integrals):
    wide = lax.axis_index("wide")
    table = jnp.asarray(place_table())[wide, lax.axis_index("layer")]

    i1 = send(integrals, (1, 0), (0, 1))
    p0 = join(integrals, i1)
    i2, i3 = send(p0, (2, 0), (0, 2)), send(p0, (0, 0), (0, -2))
    u0 = join(p0, i2)
    i4 = send(i2, (0, 0), (0, 2))
    u1 = join(i3, i4)

    low, high = prep(table, tile_count, amplitudes[:, 0, :], tile_pos.reshape(1, 128))
    left_low, right_high = shift(low, 1), shift(high, -1)
    left_high, right_low = shift(high, 1), shift(low, -1)
    far_low, far_high = shift(left_low, 1), shift(right_high, -1)

    r1p, r1m = send(u0, (0, 1), (1, 0)), send(u1, (0, -1), (-1, 0))
    r2p, r2m = send(r1p, (0, 1), (1, 0)), send(r1m, (0, -1), (-1, 0))
    r3p, r3m = send(r2p, (0, 1), (1, 0)), send(r2m, (0, -1), (-1, 0))
    r4 = send(r3p, (0, 1), None)

    mine = [u0, r1p, r1m, r2p, r2m, r3p, r3m]
    blocks = {n: (unit,) for n, unit in enumerate(mine)} | {7: (r4, u1)}
    blocks |= {8 + n: (swap(unit),) for n, unit in enumerate(mine)}
    blocks[15] = (swap(u1, (1,)), swap(r4, (0,)))

    dense = place(table, [low, high], ((0, 0), (0, 1)))
    dense = place(table, [left_low, left_high], ((3, 0), (3, 1)), dense)
    dense = place(table, [right_low, right_high], ((1, 0), (1, 1)), dense)
    dense = place(table, [far_low, far_high], ((2, 0), (2, 1)), dense)
    late = (6, 7, 14, 15)
    early = [(k, blocks[k]) for k in range(16) if k not in late]
    total = product(table, dense, early, None, jnp.float32)
    return product(table, dense, [(k, blocks[k]) for k in late], total, jnp.bfloat16)


def solution(mesh):
    in_specs = (
        P("wide", "layer", None),
        P("wide", "layer"),
        P("wide", "layer"),
        P("wide", "layer"),
    )
    return jax.shard_map(steps, mesh=mesh, in_specs=in_specs, out_specs=P("wide", "layer"), check_vma=False)
```

```python
import functools

import jax
import jax.numpy as jnp
import numpy as np
from jax import lax
from jax.experimental import pallas as pl
from jax.experimental.pallas import tpu as pltpu
from jax.sharding import PartitionSpec as P


Y, Z, CORES, LAYERS = 4, 8, 2, 4
HALF = 32 * 64
META = 16
ABSENT = 256
UNROLL = 8
MIB = 1 << 20


UNIT_BY_DZ = {0: 0, 7: 1, 1: 2, 6: 3, 2: 4, 5: 5, 3: 6, 4: 7}
PLACE_BY_DY = {0: 0, 3: 1, 2: 2, 1: 3}
HALF_BY_DZ = {0: (0, 0), 7: (0, 1), 6: (0, 2), 5: (0, 3), 2: (1, 0), 1: (1, 1), 4: (1, 2), 3: (1, 3)}
UNIT_BY_HALF_DY = {(0, 0): 0, (0, 3): 1, (0, 1): 2, (0, 2): 3, (1, 1): 4, (1, 3): 5, (1, 2): 6, (1, 0): 7}


def place_table():
    table = np.zeros((Y, Z, CORES, LAYERS, LAYERS, 16), np.int32)
    for y, z, c, x, dx, t in np.ndindex(*table.shape):
        layer = (x + dx) % LAYERS
        dy, dz, core = (layer - y) % Y, (t // 2 - z) % Z, t % 2
        if core == 0:
            unit, place = UNIT_BY_DZ[dz], PLACE_BY_DY[dy]
        else:
            half, place = HALF_BY_DZ[dz]
            unit = UNIT_BY_HALF_DY[half, dy]
        table[y, z, c, x, dx, t] = (unit + (0 if core == c else 8)) * 4 + place
    core = np.broadcast_to(np.arange(CORES, dtype=np.int32)[:, None, None, None], (Y, Z, CORES, LAYERS, 1, 16))
    return np.concatenate([table, core], axis=4).reshape(Y * Z * CORES, LAYERS, LAYERS + 1, 16)


def vmem():
    return pl.BlockSpec(memory_space=pltpu.VMEM)


def smem():
    return pl.BlockSpec(memory_space=pltpu.SMEM)


def prep_kernel(table_ref, count_ref, amp_ref, pos_ref, low_ref, high_ref, wide_ref):
    left = lax.broadcasted_iota(jnp.int32, (64, 128), 1) < 64
    for t in range(32):
        cols = slice(t * 128, (t + 1) * 128)
        xa = amp_ref[0:64, cols].astype(jnp.float32)
        xb = amp_ref[64:128, cols].astype(jnp.float32)
        even = jnp.where(left, xa, pltpu.roll(xb, 64, 1))
        odd = jnp.where(left, pltpu.roll(xa, 64, 1), xb)
        wide_ref[2 * t * 64 : (2 * t + 1) * 64, :] = even
        wide_ref[(2 * t + 1) * 64 : (2 * t + 2) * 64, :] = odd
    slot = lax.broadcasted_iota(jnp.int32, (1, 128), 1)
    code = jnp.where(slot < count_ref[0, 0], pos_ref[...], ABSENT).astype(jnp.float32)
    code = jnp.broadcast_to(code, (META, 128)).astype(jnp.bfloat16)
    for half, ref in enumerate((low_ref, high_ref)):
        for s in range(32):
            rows = wide_ref[pl.ds(half * 32 + s, 64, stride=64), :]
            ref[s * 64 : (s + 1) * 64, :] = rows.astype(jnp.bfloat16)
        ref[HALF:, :] = code


def prep(table, count, amplitudes, positions):
    out = jax.ShapeDtypeStruct((HALF + META, 128), jnp.bfloat16)
    return pl.pallas_call(
        prep_kernel,
        out_shape=(out, out),
        in_specs=[smem(), smem(), vmem(), vmem()],
        out_specs=(vmem(), vmem()),
        scratch_shapes=[pltpu.VMEM((4096, 128), jnp.float32)],
        compiler_params=pltpu.CompilerParams(vmem_limit_bytes=6 * MIB),
        name="prep",
    )(table, count, amplitudes, positions)


def join_kernel(a_ref, b_ref, out_ref):
    out_ref[: a_ref.shape[0]] = a_ref[...]
    out_ref[a_ref.shape[0] :] = b_ref[...]


def join(a, b):
    out = pl.pallas_call(
        join_kernel,
        out_shape=jax.ShapeDtypeStruct((a.shape[0] + b.shape[0], a.shape[1]), a.dtype),
        in_specs=[vmem(), vmem()],
        out_specs=vmem(),
        compiler_params=pltpu.CompilerParams(vmem_limit_bytes=2 * MIB),
        name="join",
    )(a, b)
    return out


def pick_kernel(table_ref, whole_ref, a_ref, b_ref, out_ref):
    @pl.when(table_ref[LAYERS, 0] == 0)
    def _():
        out_ref[...] = whole_ref[...]

    @pl.when(table_ref[LAYERS, 0] == 1)
    def _():
        join_kernel(a_ref, b_ref, out_ref)


def pick(table, whole, a, b):
    return pl.pallas_call(
        pick_kernel,
        out_shape=jax.ShapeDtypeStruct(whole.shape, whole.dtype),
        in_specs=[smem(), vmem(), vmem(), vmem()],
        out_specs=vmem(),
        compiler_params=pltpu.CompilerParams(vmem_limit_bytes=2 * MIB),
        name="pick",
    )(table, whole, a, b)


def choose_kernel(table_ref, a_ref, b_ref, out_ref):
    for core, ref in enumerate((a_ref, b_ref)):

        @pl.when(table_ref[LAYERS, 0] == core)
        def _():
            out_ref[...] = ref[...]


def choose(table, a, b):
    return pl.pallas_call(
        choose_kernel,
        out_shape=jax.ShapeDtypeStruct(a.shape, a.dtype),
        in_specs=[smem(), vmem(), vmem()],
        out_specs=vmem(),
        compiler_params=pltpu.CompilerParams(vmem_limit_bytes=2 * MIB),
        name="choose",
    )(table, a, b)


def place_kernel(halves, given, table_ref, *refs):
    sources, rest = refs[: len(halves)], refs[len(halves) :]
    if given:
        dense_ref, _, code_v, code_s, sem = rest
    else:
        dense_ref, code_v, code_s, sem = rest

        def zero(k, carry):
            dense_ref[k] = jnp.zeros((1024, 128), jnp.bfloat16)
            return carry

        lax.fori_loop(0, 32, zero, 0)
    side = jnp.where(lax.broadcasted_iota(jnp.int32, (64, 128), 1) < 64, 0, 1)
    for n, source_ref in enumerate(sources):
        code_v[8 * n : 8 * n + 8] = source_ref[HALF:, :].astype(jnp.float32).astype(jnp.int32)[0:8]
    copy = pltpu.make_async_copy(code_v, code_s, sem)
    copy.start()
    copy.wait()
    for n, (source_ref, (piece, half)) in enumerate(zip(sources, halves)):

        def trip(first, carry):
            for j in range(UNROLL):
                s = first * UNROLL + j
                block = source_ref[pl.ds(pl.multiple_of(s * 64, 64), 64), :]
                swapped = jnp.concatenate([block[:, 64:], block[:, :64]], axis=1)
                for h in range(2):
                    code = code_s[8 * n, h * 64 + half * 32 + s]
                    u = table_ref[piece, code & 15]
                    q = u & 1
                    tile = jnp.where(q == h, block, swapped)
                    k = jnp.where(code < ABSENT, u >> 1, 32)
                    rows = pl.ds(pl.multiple_of((code & 240) * 4, 64), 64)
                    dense_ref[k, rows, :] = jnp.where(side == q, tile, dense_ref[k, rows, :])
            return carry

        lax.fori_loop(0, 32 // UNROLL, trip, 0)


def place(table, sources, halves, dense=None):
    given = [] if dense is None else [dense]
    n = len(sources)
    out = pl.pallas_call(
        functools.partial(place_kernel, halves, bool(given)),
        out_shape=jax.ShapeDtypeStruct((33, 1024, 128), jnp.bfloat16),
        in_specs=[smem()] + [vmem()] * (n + len(given)),
        out_specs=vmem(),
        input_output_aliases={n + 1: 0} if given else {},
        scratch_shapes=[
            pltpu.VMEM((8 * n, 128), jnp.int32),
            pltpu.SMEM((8 * n, 128), jnp.int32),
            pltpu.SemaphoreType.DMA,
        ],
        compiler_params=pltpu.CompilerParams(vmem_limit_bytes=16 * MIB),
        name="place",
    )(table, *sources, *given)
    return out


def product_kernel(units, table_ref, dense_ref, *refs):
    out_ref, chosen_ref = refs[-2:]
    blocks, at, slot = [], 0, 0
    for k, choices in units:
        if choices == 1:
            blocks.append((k, refs[at]))
        else:
            choose_kernel(table_ref, refs[at], refs[at + 1], chosen_ref.at[slot])
            blocks.append((k, chosen_ref.at[slot]))
            slot += 1
        at += choices

    def rows_of(i, carry):
        rows = pl.ds(pl.multiple_of(i * 512, 512), 512)
        for n in range(4):
            cols = slice(n * 256, (n + 1) * 256)
            total = None
            for k, block in blocks:
                left = jnp.concatenate([dense_ref[2 * k, rows, :], dense_ref[2 * k + 1, rows, :]], axis=1)
                part = jnp.dot(left, block[:, cols], preferred_element_type=jnp.float32)
                total = part if total is None else total + part
            out_ref[rows, cols] = total.astype(out_ref.dtype)
        return carry

    lax.fori_loop(0, 2, rows_of, 0)


def product(table, dense, blocks):
    arrays = [array for _, choices in blocks for array in choices]
    units = tuple((k, len(choices)) for k, choices in blocks)
    return pl.pallas_call(
        functools.partial(product_kernel, units),
        out_shape=jax.ShapeDtypeStruct((1024, 1024), jnp.bfloat16),
        in_specs=[smem()] + [vmem()] * (1 + len(arrays)),
        out_specs=vmem(),
        scratch_shapes=[pltpu.VMEM((2, 256, 1024), jnp.bfloat16)],
        compiler_params=pltpu.CompilerParams(vmem_limit_bytes=16 * MIB),
        name="product",
    )(table, dense, *arrays)


def pairs(move0, move1):
    out = []
    for y, z, c in np.ndindex(Y, Z, CORES):
        move = (move0, move1)[c]
        if move is not None:
            target = ((y + move[0]) % Y * Z + (z + move[1]) % Z) * CORES + c
            out.append(((y * Z + z) * CORES + c, int(target)))
    return out


def send(value, move0, move1):
    return lax.ppermute(value, "wide", pairs(move0, move1))


def swap(value, cores=(0, 1)):
    return lax.ppermute(value, "wide", [(i, i ^ 1) for i in range(Y * Z * CORES) if i % 2 in cores])


def shift(value, step):
    return lax.ppermute(value, "layer", [(i, (i + step) % LAYERS) for i in range(LAYERS)])


def steps(amplitudes, tile_pos, tile_count, integrals):
    wide = lax.axis_index("wide")
    table = jnp.asarray(place_table())[wide, lax.axis_index("layer")]

    i1 = send(integrals, (1, 0), (0, 1))
    low, high = prep(table, tile_count, amplitudes[:, 0, :], tile_pos.reshape(1, 128))
    p0 = join(integrals, i1)
    i2, i3 = send(p0, (2, 0), (0, 2)), send(p0, None, (0, -2))
    u0 = join(p0, i2)
    i4 = send(i3, None, (0, -2))

    left_low, right_high = shift(low, 1), shift(high, -1)
    left_high, right_low = shift(high, 1), shift(low, -1)
    far_low, far_high = shift(left_low, 1), shift(right_high, -1)

    r1p, r1m = send(u0, (0, 1), (1, 0)), send(u0, (0, -1), (-1, 0))
    w2 = pick(table, r1m, i3, i4)
    r2p, r2m = send(r1p, (0, 1), (1, 0)), send(w2, (0, -1), (-1, 0))
    w3 = choose(table, r2p, w2)
    r3p, r3m = send(w3, (0, 1), (1, 0)), send(r2m, (0, -1), (-1, 0))
    r4 = send(r3p, (0, 1), None)

    mine = [u0, r1p, r1m, r2p, r2m, r3p, r3m]
    blocks = {n: (unit,) for n, unit in enumerate(mine)} | {7: (r4, w2)}
    blocks |= {8 + n: (swap(unit),) for n, unit in enumerate(mine)}
    blocks[15] = (swap(w2, (1,)), swap(r4, (0,)))

    dense = place(table, [low, high], ((0, 0), (0, 1)))
    dense = place(table, [left_low, left_high], ((3, 0), (3, 1)), dense)
    dense = place(table, [right_low, right_high], ((1, 0), (1, 1)), dense)
    dense = place(table, [far_low, far_high], ((2, 0), (2, 1)), dense)
    return product(table, dense, [(k, blocks[k]) for n in range(8) for k in (n, 8 + n)])


def solution(mesh):
    in_specs = (
        P("wide", "layer", None),
        P("wide", "layer"),
        P("wide", "layer"),
        P("wide", "layer"),
    )
    return jax.shard_map(steps, mesh=mesh, in_specs=in_specs, out_specs=P("wide", "layer"), check_vma=False)
```

```python
import functools

import jax
import jax.numpy as jnp
import numpy as np
from jax import lax
from jax.experimental import pallas as pl
from jax.experimental.pallas import tpu as pltpu
from jax.sharding import PartitionSpec as P


Y, Z, CORES, LAYERS = 4, 8, 2, 4
HALF = 32 * 64
META = 16
ABSENT = 256
UNROLL = 8
MIB = 1 << 20


UNIT_BY_DZ = {0: 0, 7: 1, 1: 2, 6: 3, 2: 4, 5: 5, 3: 6, 4: 7}
PLACE_BY_DY = {0: 0, 3: 1, 2: 2, 1: 3}
HALF_BY_DZ = {0: (0, 0), 7: (0, 1), 6: (0, 2), 5: (0, 3), 2: (1, 0), 1: (1, 1), 4: (1, 2), 3: (1, 3)}
UNIT_BY_HALF_DY = {(0, 0): 0, (0, 3): 1, (0, 1): 2, (0, 2): 3, (1, 1): 4, (1, 3): 5, (1, 2): 6, (1, 0): 7}


def place_table():
    table = np.zeros((Y, Z, CORES, LAYERS, LAYERS, 16), np.int32)
    for y, z, c, x, dx, t in np.ndindex(*table.shape):
        layer = (x + dx) % LAYERS
        dy, dz, core = (layer - y) % Y, (t // 2 - z) % Z, t % 2
        if core == 0:
            unit, place = UNIT_BY_DZ[dz], PLACE_BY_DY[dy]
        else:
            half, place = HALF_BY_DZ[dz]
            unit = UNIT_BY_HALF_DY[half, dy]
        table[y, z, c, x, dx, t] = (unit + (0 if core == c else 8)) * 4 + place
    core = np.broadcast_to(np.arange(CORES, dtype=np.int32)[:, None, None, None], (Y, Z, CORES, LAYERS, 1, 16))
    return np.concatenate([table, core], axis=4).reshape(Y * Z * CORES, LAYERS, LAYERS + 1, 16)


def vmem():
    return pl.BlockSpec(memory_space=pltpu.VMEM)


def smem():
    return pl.BlockSpec(memory_space=pltpu.SMEM)


def prep_kernel(table_ref, count_ref, amp_ref, pos_ref, low_ref, high_ref, wide_ref):
    left = lax.broadcasted_iota(jnp.int32, (64, 128), 1) < 64
    for t in range(32):
        cols = slice(t * 128, (t + 1) * 128)
        xa = amp_ref[0:64, cols].astype(jnp.float32)
        xb = amp_ref[64:128, cols].astype(jnp.float32)
        even = jnp.where(left, xa, pltpu.roll(xb, 64, 1))
        odd = jnp.where(left, pltpu.roll(xa, 64, 1), xb)
        wide_ref[2 * t * 64 : (2 * t + 1) * 64, :] = even
        wide_ref[(2 * t + 1) * 64 : (2 * t + 2) * 64, :] = odd
    slot = lax.broadcasted_iota(jnp.int32, (1, 128), 1)
    code = jnp.where(slot < count_ref[0, 0], pos_ref[...], ABSENT).astype(jnp.float32)
    code = jnp.broadcast_to(code, (META, 128)).astype(jnp.bfloat16)
    for half, ref in enumerate((low_ref, high_ref)):
        for s in range(32):
            rows = wide_ref[pl.ds(half * 32 + s, 64, stride=64), :]
            ref[s * 64 : (s + 1) * 64, :] = rows.astype(jnp.bfloat16)
        ref[HALF:, :] = code


def prep(table, count, amplitudes, positions):
    out = jax.ShapeDtypeStruct((HALF + META, 128), jnp.bfloat16)
    return pl.pallas_call(
        prep_kernel,
        out_shape=(out, out),
        in_specs=[smem(), smem(), vmem(), vmem()],
        out_specs=(vmem(), vmem()),
        scratch_shapes=[pltpu.VMEM((4096, 128), jnp.float32)],
        compiler_params=pltpu.CompilerParams(vmem_limit_bytes=6 * MIB),
        name="prep",
    )(table, count, amplitudes, positions)


def join_kernel(a_ref, b_ref, out_ref):
    out_ref[: a_ref.shape[0]] = a_ref[...]
    out_ref[a_ref.shape[0] :] = b_ref[...]


def join(a, b):
    out = pl.pallas_call(
        join_kernel,
        out_shape=jax.ShapeDtypeStruct((a.shape[0] + b.shape[0], a.shape[1]), a.dtype),
        in_specs=[vmem(), vmem()],
        out_specs=vmem(),
        compiler_params=pltpu.CompilerParams(vmem_limit_bytes=2 * MIB),
        name="join",
    )(a, b)
    return out


def pick_kernel(table_ref, whole_ref, a_ref, b_ref, out_ref):
    @pl.when(table_ref[LAYERS, 0] == 0)
    def _():
        out_ref[...] = whole_ref[...]

    @pl.when(table_ref[LAYERS, 0] == 1)
    def _():
        join_kernel(a_ref, b_ref, out_ref)


def pick(table, whole, a, b):
    return pl.pallas_call(
        pick_kernel,
        out_shape=jax.ShapeDtypeStruct(whole.shape, whole.dtype),
        in_specs=[smem(), vmem(), vmem(), vmem()],
        out_specs=vmem(),
        compiler_params=pltpu.CompilerParams(vmem_limit_bytes=2 * MIB),
        name="pick",
    )(table, whole, a, b)


def choose_kernel(table_ref, a_ref, b_ref, out_ref):
    for core, ref in enumerate((a_ref, b_ref)):

        @pl.when(table_ref[LAYERS, 0] == core)
        def _():
            out_ref[...] = ref[...]


def choose(table, a, b):
    return pl.pallas_call(
        choose_kernel,
        out_shape=jax.ShapeDtypeStruct(a.shape, a.dtype),
        in_specs=[smem(), vmem(), vmem()],
        out_specs=vmem(),
        compiler_params=pltpu.CompilerParams(vmem_limit_bytes=2 * MIB),
        name="choose",
    )(table, a, b)


def place_kernel(halves, given, table_ref, *refs):
    sources, rest = refs[: len(halves)], refs[len(halves) :]
    if given:
        dense_ref, _, code_v, code_s, sem = rest
    else:
        dense_ref, code_v, code_s, sem = rest

        def zero(k, carry):
            dense_ref[k] = jnp.zeros((1024, 128), jnp.bfloat16)
            return carry

        lax.fori_loop(0, 32, zero, 0)
    side = jnp.where(lax.broadcasted_iota(jnp.int32, (64, 128), 1) < 64, 0, 1)
    for n, source_ref in enumerate(sources):
        code_v[8 * n : 8 * n + 8] = source_ref[HALF:, :].astype(jnp.float32).astype(jnp.int32)[0:8]
    copy = pltpu.make_async_copy(code_v, code_s, sem)
    copy.start()
    copy.wait()
    for n, (source_ref, (piece, half)) in enumerate(zip(sources, halves)):

        def trip(first, carry):
            for j in range(UNROLL):
                s = first * UNROLL + j
                block = source_ref[pl.ds(pl.multiple_of(s * 64, 64), 64), :]
                swapped = jnp.concatenate([block[:, 64:], block[:, :64]], axis=1)
                for h in range(2):
                    code = code_s[8 * n, h * 64 + half * 32 + s]
                    u = table_ref[piece, code & 15]
                    q = u & 1
                    tile = jnp.where(q == h, block, swapped)
                    k = jnp.where(code < ABSENT, u >> 1, 32)
                    rows = pl.ds(pl.multiple_of((code & 240) * 4, 64), 64)
                    dense_ref[k, rows, :] = jnp.where(side == q, tile, dense_ref[k, rows, :])
            return carry

        lax.fori_loop(0, 32 // UNROLL, trip, 0)


def place(table, sources, halves, dense=None):
    given = [] if dense is None else [dense]
    n = len(sources)
    out = pl.pallas_call(
        functools.partial(place_kernel, halves, bool(given)),
        out_shape=jax.ShapeDtypeStruct((33, 1024, 128), jnp.bfloat16),
        in_specs=[smem()] + [vmem()] * (n + len(given)),
        out_specs=vmem(),
        input_output_aliases={n + 1: 0} if given else {},
        scratch_shapes=[
            pltpu.VMEM((8 * n, 128), jnp.int32),
            pltpu.SMEM((8 * n, 128), jnp.int32),
            pltpu.SemaphoreType.DMA,
        ],
        compiler_params=pltpu.CompilerParams(vmem_limit_bytes=16 * MIB),
        name="place",
    )(table, *sources, *given)
    return out


def product_kernel(units, has_total, table_ref, dense_ref, *refs):
    out_ref, chosen_ref = refs[-2:]
    blocks, at, slot = [], 0, 0
    for k, choices in units:
        if choices == 1:
            blocks.append((k, refs[at]))
        else:
            choose_kernel(table_ref, refs[at], refs[at + 1], chosen_ref.at[slot])
            blocks.append((k, chosen_ref.at[slot]))
            slot += 1
        at += choices

    def rows_of(i, carry):
        rows = pl.ds(pl.multiple_of(i * 512, 512), 512)
        for n in range(4):
            cols = slice(n * 256, (n + 1) * 256)
            total = refs[-3][rows, cols] if has_total else None
            for k, block in blocks:
                left = jnp.concatenate([dense_ref[2 * k, rows, :], dense_ref[2 * k + 1, rows, :]], axis=1)
                part = jnp.dot(left, block[:, cols], preferred_element_type=jnp.float32)
                total = part if total is None else total + part
            out_ref[rows, cols] = total.astype(out_ref.dtype)
        return carry

    lax.fori_loop(0, 2, rows_of, 0)


def product(table, dense, blocks, total, dtype):
    arrays = [array for _, choices in blocks for array in choices]
    units = tuple((k, len(choices)) for k, choices in blocks)
    totals = [] if total is None else [total]
    return pl.pallas_call(
        functools.partial(product_kernel, units, bool(totals)),
        out_shape=jax.ShapeDtypeStruct((1024, 1024), dtype),
        in_specs=[smem()] + [vmem()] * (1 + len(arrays) + len(totals)),
        out_specs=vmem(),
        scratch_shapes=[pltpu.VMEM((2, 256, 1024), jnp.bfloat16)],
        compiler_params=pltpu.CompilerParams(vmem_limit_bytes=16 * MIB),
        name="product",
    )(table, dense, *arrays, *totals)


def pairs(move0, move1):
    out = []
    for y, z, c in np.ndindex(Y, Z, CORES):
        move = (move0, move1)[c]
        if move is not None:
            target = ((y + move[0]) % Y * Z + (z + move[1]) % Z) * CORES + c
            out.append(((y * Z + z) * CORES + c, int(target)))
    return out


def send(value, move0, move1):
    return lax.ppermute(value, "wide", pairs(move0, move1))


def swap(value, cores=(0, 1)):
    return lax.ppermute(value, "wide", [(i, i ^ 1) for i in range(Y * Z * CORES) if i % 2 in cores])


def shift(value, step):
    return lax.ppermute(value, "layer", [(i, (i + step) % LAYERS) for i in range(LAYERS)])


def steps(amplitudes, tile_pos, tile_count, integrals):
    wide = lax.axis_index("wide")
    table = jnp.asarray(place_table())[wide, lax.axis_index("layer")]

    i1 = send(integrals, (1, 0), (0, 1))
    low, high = prep(table, tile_count, amplitudes[:, 0, :], tile_pos.reshape(1, 128))
    p0 = join(integrals, i1)
    i2, i3 = send(p0, (2, 0), (0, 2)), send(p0, None, (0, -2))
    u0 = join(p0, i2)
    i4 = send(i3, None, (0, -2))

    left_low, right_high = shift(low, 1), shift(high, -1)
    left_high, right_low = shift(high, 1), shift(low, -1)
    far_low, far_high = shift(left_low, 1), shift(right_high, -1)

    r1p, r1m = send(u0, (0, 1), (1, 0)), send(u0, (0, -1), (-1, 0))
    w2 = pick(table, r1m, i3, i4)
    r2p, r2m = send(r1p, (0, 1), (1, 0)), send(w2, (0, -1), (-1, 0))
    w3 = choose(table, r2p, w2)
    r3p, r3m = send(w3, (0, 1), (1, 0)), send(r2m, (0, -1), (-1, 0))
    r4 = send(r3p, (0, 1), None)

    mine = [u0, r1p, r1m, r2p, r2m, r3p, r3m]
    blocks = {n: (unit,) for n, unit in enumerate(mine)} | {7: (r4, w2)}
    blocks |= {8 + n: (swap(unit),) for n, unit in enumerate(mine)}
    blocks[15] = (swap(w2, (1,)), swap(r4, (0,)))

    dense = place(table, [low, high], ((0, 0), (0, 1)))
    dense = place(table, [left_low, left_high], ((3, 0), (3, 1)), dense)
    dense = place(table, [right_low, right_high], ((1, 0), (1, 1)), dense)
    dense = place(table, [far_low, far_high], ((2, 0), (2, 1)), dense)
    early, late = (0, 1, 2, 3, 4), (5, 6, 7)
    total = product(table, dense, [(k, blocks[k]) for n in early for k in (n, 8 + n)], None, jnp.float32)
    return product(table, dense, [(k, blocks[k]) for n in late for k in (n, 8 + n)], total, jnp.bfloat16)


def solution(mesh):
    in_specs = (
        P("wide", "layer", None),
        P("wide", "layer"),
        P("wide", "layer"),
        P("wide", "layer"),
    )
    return jax.shard_map(steps, mesh=mesh, in_specs=in_specs, out_specs=P("wide", "layer"), check_vma=False)
```

```python
import functools

import jax
import jax.numpy as jnp
import numpy as np
from jax import lax
from jax.experimental import pallas as pl
from jax.experimental.pallas import tpu as pltpu
from jax.sharding import PartitionSpec as P


Y, Z, CORES, LAYERS = 4, 8, 2, 4
HALF = 32 * 64
META = 16
ABSENT = 256
UNROLL = 32
MIB = 1 << 20


UNIT_BY_DZ = {0: 0, 7: 1, 1: 2, 6: 3, 2: 4, 5: 5, 3: 6, 4: 7}
PLACE_BY_DY = {0: 0, 3: 1, 2: 2, 1: 3}
HALF_BY_DZ = {0: (0, 0), 7: (0, 1), 6: (0, 2), 5: (0, 3), 2: (1, 0), 1: (1, 1), 4: (1, 2), 3: (1, 3)}
UNIT_BY_HALF_DY = {(0, 0): 0, (0, 3): 1, (0, 1): 2, (0, 2): 3, (1, 1): 4, (1, 3): 5, (1, 2): 6, (1, 0): 7}


def place_table():
    table = np.zeros((Y, Z, CORES, LAYERS, LAYERS, 16), np.int32)
    for y, z, c, x, dx, t in np.ndindex(*table.shape):
        layer = (x + dx) % LAYERS
        dy, dz, core = (layer - y) % Y, (t // 2 - z) % Z, t % 2
        if core == 0:
            unit, place = UNIT_BY_DZ[dz], PLACE_BY_DY[dy]
        else:
            half, place = HALF_BY_DZ[dz]
            unit = UNIT_BY_HALF_DY[half, dy]
        table[y, z, c, x, dx, t] = (unit + (0 if core == c else 8)) * 4 + place
    core = np.broadcast_to(np.arange(CORES, dtype=np.int32)[:, None, None, None], (Y, Z, CORES, LAYERS, 1, 16))
    return np.concatenate([table, core], axis=4).reshape(Y * Z * CORES, LAYERS, LAYERS + 1, 16)


def vmem():
    return pl.BlockSpec(memory_space=pltpu.VMEM)


def smem():
    return pl.BlockSpec(memory_space=pltpu.SMEM)


def prep_kernel(table_ref, count_ref, amp_ref, pos_ref, low_ref, high_ref, wide_ref):
    left = lax.broadcasted_iota(jnp.int32, (64, 128), 1) < 64
    for t in range(32):
        cols = slice(t * 128, (t + 1) * 128)
        xa = amp_ref[0:64, cols].astype(jnp.float32)
        xb = amp_ref[64:128, cols].astype(jnp.float32)
        even = jnp.where(left, xa, pltpu.roll(xb, 64, 1))
        odd = jnp.where(left, pltpu.roll(xa, 64, 1), xb)
        wide_ref[2 * t * 64 : (2 * t + 1) * 64, :] = even
        wide_ref[(2 * t + 1) * 64 : (2 * t + 2) * 64, :] = odd
    slot = lax.broadcasted_iota(jnp.int32, (1, 128), 1)
    code = jnp.where(slot < count_ref[0, 0], pos_ref[...], ABSENT).astype(jnp.float32)
    code = jnp.broadcast_to(code, (META, 128)).astype(jnp.bfloat16)
    for half, ref in enumerate((low_ref, high_ref)):
        for s in range(32):
            rows = wide_ref[pl.ds(half * 32 + s, 64, stride=64), :]
            ref[s * 64 : (s + 1) * 64, :] = rows.astype(jnp.bfloat16)
        ref[HALF:, :] = code


def prep(table, count, amplitudes, positions):
    out = jax.ShapeDtypeStruct((HALF + META, 128), jnp.bfloat16)
    return pl.pallas_call(
        prep_kernel,
        out_shape=(out, out),
        in_specs=[smem(), smem(), vmem(), vmem()],
        out_specs=(vmem(), vmem()),
        scratch_shapes=[pltpu.VMEM((4096, 128), jnp.float32)],
        compiler_params=pltpu.CompilerParams(vmem_limit_bytes=6 * MIB),
        name="prep",
    )(table, count, amplitudes, positions)


def join_kernel(a_ref, b_ref, out_ref):
    out_ref[: a_ref.shape[0]] = a_ref[...]
    out_ref[a_ref.shape[0] :] = b_ref[...]


def join(a, b):
    out = pl.pallas_call(
        join_kernel,
        out_shape=jax.ShapeDtypeStruct((a.shape[0] + b.shape[0], a.shape[1]), a.dtype),
        in_specs=[vmem(), vmem()],
        out_specs=vmem(),
        compiler_params=pltpu.CompilerParams(vmem_limit_bytes=2 * MIB),
        name="join",
    )(a, b)
    return out


def pick_kernel(table_ref, whole_ref, a_ref, b_ref, out_ref):
    @pl.when(table_ref[LAYERS, 0] == 0)
    def _():
        out_ref[...] = whole_ref[...]

    @pl.when(table_ref[LAYERS, 0] == 1)
    def _():
        join_kernel(a_ref, b_ref, out_ref)


def pick(table, whole, a, b):
    return pl.pallas_call(
        pick_kernel,
        out_shape=jax.ShapeDtypeStruct(whole.shape, whole.dtype),
        in_specs=[smem(), vmem(), vmem(), vmem()],
        out_specs=vmem(),
        compiler_params=pltpu.CompilerParams(vmem_limit_bytes=2 * MIB),
        name="pick",
    )(table, whole, a, b)


def choose_kernel(table_ref, a_ref, b_ref, out_ref):
    for core, ref in enumerate((a_ref, b_ref)):

        @pl.when(table_ref[LAYERS, 0] == core)
        def _():
            out_ref[...] = ref[...]


def choose(table, a, b):
    return pl.pallas_call(
        choose_kernel,
        out_shape=jax.ShapeDtypeStruct(a.shape, a.dtype),
        in_specs=[smem(), vmem(), vmem()],
        out_specs=vmem(),
        compiler_params=pltpu.CompilerParams(vmem_limit_bytes=2 * MIB),
        name="choose",
    )(table, a, b)


def place_kernel(halves, given, table_ref, *refs):
    sources, rest = refs[: len(halves)], refs[len(halves) :]
    if given:
        dense_ref, _, code_v, code_s, sem = rest
    else:
        dense_ref, code_v, code_s, sem = rest

        def zero(k, carry):
            dense_ref[k] = jnp.zeros((1024, 128), jnp.bfloat16)
            return carry

        lax.fori_loop(0, 32, zero, 0)
    side = jnp.where(lax.broadcasted_iota(jnp.int32, (64, 128), 1) < 64, 0, 1)
    for n, source_ref in enumerate(sources):
        code_v[8 * n : 8 * n + 8] = source_ref[HALF:, :].astype(jnp.float32).astype(jnp.int32)[0:8]
    copy = pltpu.make_async_copy(code_v, code_s, sem)
    copy.start()
    copy.wait()
    for n, (source_ref, (piece, half)) in enumerate(zip(sources, halves)):

        def trip(first, carry):
            for j in range(UNROLL):
                s = first * UNROLL + j
                block = source_ref[pl.ds(pl.multiple_of(s * 64, 64), 64), :]
                swapped = jnp.concatenate([block[:, 64:], block[:, :64]], axis=1)
                for h in range(2):
                    code = code_s[8 * n, h * 64 + half * 32 + s]
                    u = table_ref[piece, code & 15]
                    q = u & 1
                    tile = jnp.where(q == h, block, swapped)
                    k = jnp.where(code < ABSENT, u >> 1, 32)
                    rows = pl.ds(pl.multiple_of((code & 240) * 4, 64), 64)
                    dense_ref[k, rows, :] = jnp.where(side == q, tile, dense_ref[k, rows, :])
            return carry

        lax.fori_loop(0, 32 // UNROLL, trip, 0)


def place(table, sources, halves, dense=None):
    given = [] if dense is None else [dense]
    n = len(sources)
    out = pl.pallas_call(
        functools.partial(place_kernel, halves, bool(given)),
        out_shape=jax.ShapeDtypeStruct((33, 1024, 128), jnp.bfloat16),
        in_specs=[smem()] + [vmem()] * (n + len(given)),
        out_specs=vmem(),
        input_output_aliases={n + 1: 0} if given else {},
        scratch_shapes=[
            pltpu.VMEM((8 * n, 128), jnp.int32),
            pltpu.SMEM((8 * n, 128), jnp.int32),
            pltpu.SemaphoreType.DMA,
        ],
        compiler_params=pltpu.CompilerParams(vmem_limit_bytes=16 * MIB),
        name="place",
    )(table, *sources, *given)
    return out


def product_kernel(units, has_total, table_ref, dense_ref, *refs):
    out_ref, chosen_ref = refs[-2:]
    first = pl.program_id(0) == 0
    rows = pl.ds(pl.multiple_of(pl.program_id(0) * 512, 512), 512)
    blocks, at, slot = [], 0, 0
    for k, choices in units:
        if choices == 1:
            blocks.append((k, refs[at]))
        else:
            pl.when(first)(functools.partial(choose_kernel, table_ref, refs[at], refs[at + 1], chosen_ref.at[slot]))
            blocks.append((k, chosen_ref.at[slot]))
            slot += 1
        at += choices
    out_rows = rows if out_ref.shape[0] > 512 else slice(None)
    for n in range(4):
        cols = slice(n * 256, (n + 1) * 256)
        total = refs[-3][rows, cols] if has_total else None
        for k, block in blocks:
            left = jnp.concatenate([dense_ref[2 * k, rows, :], dense_ref[2 * k + 1, rows, :]], axis=1)
            part = jnp.dot(left, block[:, cols], preferred_element_type=jnp.float32)
            total = part if total is None else total + part
        out_ref[out_rows, cols] = total.astype(out_ref.dtype)


def product(table, dense, blocks, total, dtype):
    arrays = [array for _, choices in blocks for array in choices]
    units = tuple((k, len(choices)) for k, choices in blocks)
    totals = [] if total is None else [total]
    last = dtype == jnp.bfloat16
    return pl.pallas_call(
        functools.partial(product_kernel, units, bool(totals)),
        grid=(2,),
        out_shape=jax.ShapeDtypeStruct((1024, 1024), dtype),
        in_specs=[smem()] + [vmem()] * (1 + len(arrays) + len(totals)),
        out_specs=pl.BlockSpec((512, 1024), lambda i: (i, 0)) if last else vmem(),
        scratch_shapes=[pltpu.VMEM((2, 256, 1024), jnp.bfloat16)],
        compiler_params=pltpu.CompilerParams(vmem_limit_bytes=16 * MIB),
        name="product",
    )(table, dense, *arrays, *totals)


def pairs(move0, move1):
    out = []
    for y, z, c in np.ndindex(Y, Z, CORES):
        move = (move0, move1)[c]
        if move is not None:
            target = ((y + move[0]) % Y * Z + (z + move[1]) % Z) * CORES + c
            out.append(((y * Z + z) * CORES + c, int(target)))
    return out


def send(value, move0, move1):
    return lax.ppermute(value, "wide", pairs(move0, move1))


def swap(value, cores=(0, 1)):
    return lax.ppermute(value, "wide", [(i, i ^ 1) for i in range(Y * Z * CORES) if i % 2 in cores])


def shift(value, step):
    return lax.ppermute(value, "layer", [(i, (i + step) % LAYERS) for i in range(LAYERS)])


def steps(amplitudes, tile_pos, tile_count, integrals):
    wide = lax.axis_index("wide")
    table = jnp.asarray(place_table())[wide, lax.axis_index("layer")]

    i1 = send(integrals, (1, 0), (0, 1))
    low, high = prep(table, tile_count, amplitudes[:, 0, :], tile_pos.reshape(1, 128))
    p0 = join(integrals, i1)
    i2, i3 = send(p0, (2, 0), (0, 2)), send(p0, None, (0, -2))
    u0 = join(p0, i2)
    i4 = send(i3, None, (0, -2))

    left_low, right_high = shift(low, 1), shift(high, -1)
    left_high, right_low = shift(high, 1), shift(low, -1)
    far_low, far_high = shift(left_low, 1), shift(right_high, -1)

    r1p, r1m = send(u0, (0, 1), (1, 0)), send(u0, (0, -1), (-1, 0))
    w2 = pick(table, r1m, i3, i4)
    r2p, r2m = send(r1p, (0, 1), (1, 0)), send(w2, (0, -1), (-1, 0))
    w3 = choose(table, r2p, w2)
    r3p, r3m = send(w3, (0, 1), (1, 0)), send(r2m, (0, -1), (-1, 0))
    r4 = send(r3p, (0, 1), None)

    mine = [u0, r1p, r1m, r2p, r2m, r3p, r3m]
    blocks = {n: (unit,) for n, unit in enumerate(mine)} | {7: (r4, w2)}
    blocks |= {8 + n: (swap(unit),) for n, unit in enumerate(mine)}
    blocks[15] = (swap(w2, (1,)), swap(r4, (0,)))

    dense = place(table, [low, high], ((0, 0), (0, 1)))
    dense = place(table, [left_low, left_high], ((3, 0), (3, 1)), dense)
    dense = place(table, [right_low, right_high], ((1, 0), (1, 1)), dense)
    dense = place(table, [far_low, far_high], ((2, 0), (2, 1)), dense)
    total = None
    for part, units in ((1, (0, 1, 2, 3)), (2, (4, 5)), (3, (6, 7))):
        chosen = [(k, blocks[k]) for n in units for k in (n, 8 + n)]
        total = product(table, dense, chosen, total, jnp.bfloat16 if part == 3 else jnp.float32)
    return total


def solution(mesh):
    in_specs = (
        P("wide", "layer", None),
        P("wide", "layer"),
        P("wide", "layer"),
        P("wide", "layer"),
    )
    return jax.shard_map(steps, mesh=mesh, in_specs=in_specs, out_specs=P("wide", "layer"), check_vma=False)
```
